128 devices in a mesh: tgt: 4 (over x), inner: 32 (over z, y, core).
Axes of the slice: x: 4, y: 4, z: 4, core: 2. Of those that a mesh axis runs over, the one named last changes fastest.
Arguments:
- near_tiles: bfloat16 [512, 1024, 1024], P(('tgt', 'inner')), may hold values from -0.1875 to 0.1875
- near_target: int32 [512], P(('tgt', 'inner')), may hold values from 0 to 7
- near_right: int32 [512], P(('tgt', 'inner')), may hold values from 0 to 31
- near_count: int32 [128], P(('tgt', 'inner')), may hold values from 1 to 4, as said below
- low_u: bfloat16 [4096, 64, 1024], P(('tgt', 'inner')), may hold values from -0.75 to 0.75
- low_v: bfloat16 [4096, 64, 1024], P(('tgt', 'inner')), may hold values from -0.1875 to 0.1875
- low_target: int32 [4096], P(('tgt', 'inner')), may hold values from 0 to 7, as said below
- low_right: int32 [4096], P(('tgt', 'inner')), may hold values from 0 to 31
- right_u: bfloat16 [1024, 64, 1024], P(('tgt', 'inner')), may hold values from -6 to 6
- right_v: bfloat16 [1024, 64, 1024], P(('tgt', 'inner')), may hold values from -0.125 to 0.125
- probe_seed: int32 [32], P('tgt'), may hold values from 1 to 29999
Outputs:
- basis_out: float32 [32, 64, 1024], P('tgt', None, 'inner')
- image_out: float32 [32, 64, 1024], P('tgt', None, 'inner')
The draws below stay inside these ranges and needn't reach their ends.
Inputs may be any that keep to these rules, and one draw needn't show every extreme that they name: `near_count`: some device holds 4 live slots. `low_target`: the 32 low-rank pairs of each device name every target tile of its group.
All inputs are finite; a program needn't handle non-finite values.
Results may differ from the reference program's by a relative error of at most 0.004.
Values may be sent and summed in bfloat16 or wider, within the bound.
No kernel may reach another device: no remote copies, remote signals or barrier semaphores. Data moves between devices by JAX's collectives and lax.ppermute only.
A program may use at most 128 MiB of HBM per device.

```python
import math
import jax
import jax.numpy as jnp
from jax import lax

B = 1024
R = 64
TILE_GRP = 8
NEAR_MAX = 4
LOW_DEV = 32
RIGHT_DEV = 8
TGT_TILES = 32
RIGHT_SEG = 32
NEAR_ALL = 512
LOW_ALL = 4096
RIGHT_ALL = 1024
N_TGT = 4
N_INNER = 32


def draw_near_count(key, part):
    dev_count = NEAR_ALL // NEAR_MAX
    first_key, second_key = jax.random.split(jax.random.fold_in(key, 11))
    counts = jax.random.randint(first_key, (dev_count,), 1, NEAR_MAX + 1)
    busiest = jax.random.randint(second_key, (), 0, dev_count)
    return jnp.where(jnp.arange(dev_count) == busiest, NEAR_MAX, counts).astype(jnp.int32)


def draw_low_target(key, part):
    dev_count = LOW_ALL // LOW_DEV
    offsets = jax.random.randint(jax.random.fold_in(key, 23), (dev_count, 1), 0, TILE_GRP)
    slot_index = jnp.arange(LOW_DEV)[None, :]
    return ((slot_index + offsets) % TILE_GRP).reshape(-1).astype(jnp.int32)


def place_ends(values, key, least, largest):
    longest = values.shape.index(max(values.shape))
    spots = []
    for shift in (0, 1):
        where = [jax.random.randint(jax.random.fold_in(key, axis), (), 0, length) for axis, length in enumerate(values.shape)]
        where[longest] = (where[longest] + shift) % values.shape[longest]
        spots.append(tuple(where))
    return values.at[spots[0]].set(least).at[spots[1]].set(largest)


def steps_of(stream_key, shape, shards, low, largest):
    def one(position, parts):
        draws = jax.random.uniform(jax.random.fold_in(jax.random.fold_in(stream_key, 6), position), (parts,), jnp.float32, low / len(shards), largest / len(shards))
        return jnp.repeat(jnp.exp(draws), shape[position] // parts).reshape((-1,) + (1,) * (len(shape) - position - 1))

    level = one(*shards[0])
    for cut in shards[1:]:
        level = level * one(*cut)
    return level


def bell_draw(own_key, dims, scale, limit, cuts=(), kind=jnp.bfloat16):
    entries = jax.random.normal(own_key, dims, jnp.float32) * scale
    if len(cuts) > 0:
        entries = steps_of(own_key, dims, cuts, -0.22, 0.18) * entries
    return jnp.clip(entries, min=-limit, max=limit).astype(kind)


def setup_inputs(seed: int = 0) -> dict:
    splits = jax.random.split(jax.random.key(seed), 12)
    near_tiles = bell_draw(splits[0], (NEAR_ALL, B, B), B ** -0.5, 0.1875, ((0, 128),))
    near_target = place_ends(jax.random.randint(splits[1], (NEAR_ALL,), 0, TILE_GRP), jax.random.fold_in(splits[1], 1), 0, TILE_GRP - 1).astype(jnp.int32)
    near_right = place_ends(jax.random.randint(splits[2], (NEAR_ALL,), 0, RIGHT_SEG), jax.random.fold_in(splits[2], 1), 0, RIGHT_SEG - 1).astype(jnp.int32)
    near_count = draw_near_count(jax.random.fold_in(splits[11], 71), 0)
    low_u = bell_draw(splits[4], (LOW_ALL, R, B), R ** -0.5, 0.75, ((0, 128),))
    low_v = bell_draw(splits[5], (LOW_ALL, R, B), B ** -0.5, 0.1875, ((0, 128),))
    low_target = draw_low_target(jax.random.fold_in(splits[11], 71), 0)
    low_right = place_ends(jax.random.randint(splits[7], (LOW_ALL,), 0, RIGHT_SEG), jax.random.fold_in(splits[7], 1), 0, RIGHT_SEG - 1).astype(jnp.int32)
    right_u = bell_draw(splits[8], (RIGHT_ALL, R, B), 1.0, 6.0, ((0, 128),))
    right_v = bell_draw(splits[9], (RIGHT_ALL, R, B), (R * N_INNER) ** -0.5, 0.125, ((0, 128),))
    probe_seed = place_ends(jax.random.randint(splits[10], (TGT_TILES,), 1, 30000), jax.random.fold_in(splits[10], 1), 1, 29999).astype(jnp.int32)
    return {"near_tiles": near_tiles, "near_target": near_target, "near_right": near_right, "near_count": near_count, "low_u": low_u, "low_v": low_v, "low_target": low_target, "low_right": low_right, "right_u": right_u, "right_v": right_v, "probe_seed": probe_seed}


HIGHEST = lax.Precision.HIGHEST

def probe_table(seeds, rank_size, order):
    shape = (seeds.shape[0], rank_size, order)
    chan = lax.broadcasted_iota(jnp.int32, shape, 1)
    place = lax.broadcasted_iota(jnp.int32, shape, 2)
    code = (seeds[:, None, None] * 9973 + place * place * 7 + place * chan * 131 + chan * chan * 17 + place * 7919 + chan * 104729) % 65521
    return ((code.astype(jnp.float32) - 32760.0) / 32768.0).astype(jnp.bfloat16)

def solve_one(chol_factor, sketch_tile):
    return jax.scipy.linalg.solve_triangular(chol_factor, sketch_tile, lower=True)

def orthonormal(sketch):
    gram = jnp.einsum('tdi,tei->tde', sketch, sketch, precision=HIGHEST)
    factor = jnp.linalg.cholesky(gram)
    return jax.vmap(solve_one)(factor, sketch)

def reference(near_tiles, near_target, near_right, near_count, low_u, low_v, low_target, low_right, right_u, right_v, probe_seed):
    dev_count = N_TGT * N_INNER
    near_blocks = near_tiles.reshape(dev_count, NEAR_MAX, B, B)
    near_tgt = near_target.reshape(dev_count, NEAR_MAX)
    near_rgt = near_right.reshape(dev_count, NEAR_MAX)
    low_u_all = low_u.reshape(dev_count, LOW_DEV, R, B)
    low_v_all = low_v.reshape(dev_count, LOW_DEV, R, B)
    low_tgt = low_target.reshape(dev_count, LOW_DEV)
    low_rgt = low_right.reshape(dev_count, LOW_DEV)
    right_u_all = right_u.reshape(N_TGT, N_INNER, RIGHT_DEV, R, B)
    right_v_all = right_v.reshape(N_TGT, N_INNER, RIGHT_DEV, R, B)
    probe_all = probe_table(probe_seed, R, B)

    def terms(device):
        group = device // N_INNER
        segment = device % N_INNER
        seg_u = jnp.take(right_u_all, segment, axis=1).reshape(N_TGT * RIGHT_DEV, R, B)
        seg_v = jnp.take(right_v_all, segment, axis=1).reshape(N_TGT * RIGHT_DEV, R, B)
        near_ub = seg_u[near_rgt[device]]
        near_vb = seg_v[near_rgt[device]]
        low_ub = seg_u[low_rgt[device]]
        low_vb = seg_v[low_rgt[device]]
        live_mask = (jnp.arange(NEAR_MAX, dtype=jnp.int32) < near_count[device]).astype(jnp.float32)
        near_left = jnp.einsum('jck,jik->jci', near_ub.astype(jnp.float32), near_blocks[device].astype(jnp.float32), precision=HIGHEST) * live_mask[:, None, None]
        mixing = jnp.einsum('jak,jck->jac', low_v_all[device].astype(jnp.float32), low_ub.astype(jnp.float32), precision=HIGHEST).astype(jnp.bfloat16)
        low_left = jnp.einsum('jac,jai->jci', mixing.astype(jnp.float32), low_u_all[device].astype(jnp.float32), precision=HIGHEST)
        left_fac = jnp.concatenate([near_left, low_left], axis=0)
        right_fac = jnp.concatenate([near_vb, low_vb], axis=0).astype(jnp.float32)
        targets = jnp.concatenate([near_tgt[device], low_tgt[device]], axis=0).astype(jnp.int32)
        onehot = (targets[:, None] == jnp.arange(TILE_GRP, dtype=jnp.int32)[None, :]).astype(jnp.float32)
        return (group, left_fac, right_fac, targets, onehot)

    def sketch_step(carried, device):
        group, left_fac, right_fac, targets, onehot = terms(device)
        probe = lax.dynamic_slice_in_dim(probe_all, group * TILE_GRP, TILE_GRP, 0)
        zeta = jnp.einsum('jck,jdk->jcd', right_fac, probe[targets].astype(jnp.float32), precision=HIGHEST)
        ypair = jnp.einsum('jcd,jci->jdi', zeta, left_fac, precision=HIGHEST)
        sketch = jnp.einsum('jt,jdi->tdi', onehot, ypair, precision=HIGHEST)
        before = lax.dynamic_slice_in_dim(carried, group * TILE_GRP, TILE_GRP, 0)
        return (lax.dynamic_update_slice_in_dim(carried, before + sketch, group * TILE_GRP, 0), None)
    devices = jnp.arange(dev_count, dtype=jnp.int32)
    zeros = jnp.zeros((TGT_TILES, R, B), jnp.float32)
    sketch_total, unused = lax.scan(sketch_step, zeros, devices)
    basis = orthonormal(sketch_total)

    def image_step(carried, device):
        group, left_fac, right_fac, targets, onehot = terms(device)
        basis_grp = lax.dynamic_slice_in_dim(basis, group * TILE_GRP, TILE_GRP, 0)
        proj = jnp.einsum('jci,jdi->jcd', left_fac, basis_grp[targets], precision=HIGHEST)
        image = jnp.einsum('jcd,jck->jdk', proj, right_fac, precision=HIGHEST)
        tile_image = jnp.einsum('jt,jdk->tdk', onehot, image, precision=HIGHEST)
        before = lax.dynamic_slice_in_dim(carried, group * TILE_GRP, TILE_GRP, 0)
        return (lax.dynamic_update_slice_in_dim(carried, before + tile_image, group * TILE_GRP, 0), None)
    image_total, unused_two = lax.scan(image_step, zeros, devices)
    return (basis * math.sqrt(B), image_total)
```

```python
import jax
import jax.numpy as jnp
from jax import lax
from jax.experimental import pallas as pl
from jax.experimental.pallas import tpu as pltpu
from jax.sharding import PartitionSpec as P


B = 1024
R = 64
MOD = 65521
N_LOW = 32
N_NEAR = 4
N_PAIR = N_LOW + N_NEAR
HALF = N_PAIR // 2
F32 = jnp.float32
BF16 = jnp.bfloat16


M_T = N_PAIR
M_COUNT = 2 * N_PAIR
M_CORE = M_COUNT + 1
M_Z = M_COUNT + 2
M_Y = M_COUNT + 3
M_S = M_COUNT + 4

SMEM = pl.BlockSpec(memory_space=pltpu.MemorySpace.SMEM)
VM = pl.BlockSpec(memory_space=pltpu.MemorySpace.VMEM)
ANY = pl.BlockSpec(memory_space=pltpu.MemorySpace.HBM)
PARAMS = pltpu.CompilerParams(vmem_limit_bytes=32 * 1024 * 1024)
SMALL = pltpu.CompilerParams(vmem_limit_bytes=12 * 1024 * 1024)


def in_hbm(*xs):
    return tuple(pltpu.with_memory_space_constraint(x, pltpu.MemorySpace.HBM) for x in xs)


def dot_nt(a, b):
    return lax.dot_general(a, b, (((1,), (1,)), ((), ())), preferred_element_type=F32)


def dot_nn(a, b):
    return lax.dot_general(a, b, (((1,), (0,)), ((), ())), preferred_element_type=F32)


def split2(x):
    hi = x.astype(BF16)
    return hi, (x - hi.astype(F32)).astype(BF16)


def zeta_kernel(req, v_ref, o0, o1, o2, o3, base, probe, tab):
    c = lax.broadcasted_iota(jnp.int32, (R, B), 0)
    i = lax.broadcasted_iota(jnp.int32, (R, B), 1)
    f = i * i * 7 + i * c * 131 + c * c * 17 + i * 7919 + c * 104729
    q = (f.astype(F32) * (1.0 / MOD)).astype(jnp.int32)
    f = f - q * MOD
    f = jnp.where(f < 0, f + MOD, f)
    f = jnp.where(f >= MOD, f - MOD, f)
    base[...] = f.astype(F32)
    v = v_ref[...].reshape(8 * R, B)
    left = lax.broadcasted_iota(jnp.int32, (4 * R, 128), 1) < R

    def batch(b, carry):
        row = b // 2
        for u in range(4):
            seed = req[row, 2 * N_PAIR + (b % 2) * 4 + u]
            shift = lax.rem(seed * 9973, MOD).astype(F32)
            code = base[...] + shift
            code = jnp.where(code >= MOD, code - MOD, code)
            probe[u * R : (u + 1) * R] = ((code - 32760.0) * (1.0 / 32768.0)).astype(BF16)
        res = dot_nt(probe[...], v)
        for ip in range(4):
            blk = res[:, ip * 128 : (ip + 1) * 128]
            rolled = pltpu.roll(blk, R, 1)
            even = jnp.where(left, blk, rolled)
            odd = jnp.where(left, rolled, blk)
            for u in range(4):
                tab[b * 4 + u, 2 * ip] = even[u * R : (u + 1) * R]
                tab[b * 4 + u, 2 * ip + 1] = odd[u * R : (u + 1) * R]
        return carry

    lax.fori_loop(0, 8, batch, 0)
    lm = lax.broadcasted_iota(jnp.int32, (R, 128), 1) < R

    def slot(p, carry):
        for q, out in enumerate((o0, o1, o2, o3)):
            ra = req[q, p] & 7
            ta = req[q, N_PAIR + p]
            rb = req[q, HALF + p] & 7
            tb = req[q, N_PAIR + HALF + p]
            out[p] = jnp.where(lm, tab[q * 8 + ta, ra], tab[q * 8 + tb, rb]).astype(BF16)
        return carry

    lax.fori_loop(0, HALF, slot, 0)


def zeta_home(req, v_own):
    out = jax.ShapeDtypeStruct((HALF, R, 128), BF16)
    return pl.pallas_call(
        zeta_kernel,
        out_shape=(out,) * 4,
        in_specs=[SMEM, VM],
        out_specs=(VM,) * 4,
        scratch_shapes=[
            pltpu.VMEM((R, B), F32),
            pltpu.VMEM((4 * R, B), BF16),
            pltpu.VMEM((32, 8, R, 128), F32),
        ],
        compiler_params=PARAMS,
        name="zeta_home",
    )(req, v_own)


PLUS_TILES = 2


def start_tile(r, own, dst, sem):
    for cond, ref, shift in own(r):

        @pl.when(cond)
        def _():
            pltpu.make_async_copy(ref.at[(r & 7) - shift], dst, sem).start()


def build_plan(meta, plan):
    def per_target(t, slot):
        def per_pair(j, at):
            hit = meta[M_T + j] == t

            @pl.when(hit)
            def _():
                plan[at] = j + 256

            return at + hit.astype(jnp.int32)

        end = lax.fori_loop(0, N_LOW, per_pair, slot)
        full = (end + 3) // 4 * 4

        @pl.when(end > slot)
        def _():
            plan[64 + slot // 4] = t

            def more(c, carry):
                plan[64 + c] = t
                return carry

            lax.fori_loop(slot // 4, full // 4, more, 0)

            def pad(i, carry):
                plan[i] = plan[end - 1] & 255
                return carry

            lax.fori_loop(end, full, pad, 0)

        return full

    plan[127] = lax.fori_loop(0, 8, per_target, 0)


def pairs_body(meta, mine, own, zbuf, lv, lu, nt, mix, lt, acc, lst, lvb, lub, ub, nb, unb, sems, nsems):
    def low(j, n):
        r = meta[j]
        hit = mine(r >> 3)

        @pl.when(hit)
        def _():
            lst[n] = j
            pltpu.make_async_copy(lv.at[j], lvb.at[n], sems.at[0, n]).start()
            start_tile(r, own, ub.at[n], sems.at[1, n])
            pltpu.make_async_copy(lu.at[j], lub.at[n], sems.at[2, n]).start()

        return n + hit.astype(jnp.int32)

    n = lax.fori_loop(0, N_LOW, low, 0)

    def near(s, m):
        r = meta[N_LOW + s]
        hit = mine(r >> 3) & (s < meta[M_COUNT])

        @pl.when(hit)
        def _():
            lst[N_LOW + m] = s
            pltpu.make_async_copy(nt.at[s], nb.at[m], nsems.at[0, m]).start()
            start_tile(r, own, unb.at[m], nsems.at[1, m])

        return m + hit.astype(jnp.int32)

    nn = lax.fori_loop(0, N_NEAR, near, 0)

    def zeta(j):
        second = j >= HALF
        blk = zbuf[meta[j] >> 3, jnp.where(second, j - HALF, j)].astype(F32)
        return jnp.where(second, pltpu.roll(blk, R, 1), blk)[:, :R].astype(BF16)

    def group(g, carry):
        for i in range(4):
            pos = g * 4 + i

            @pl.when(pos < n)
            def _():
                pltpu.make_async_copy(lv.at[0], lvb.at[pos], sems.at[0, pos]).wait()
                pltpu.make_async_copy(lv.at[0], ub.at[pos], sems.at[1, pos]).wait()
                pltpu.make_async_copy(lu.at[0], lub.at[pos], sems.at[2, pos]).wait()

        for i in range(4):
            valid = (g * 4 + i < n).astype(F32)
            pos = jnp.minimum(g * 4 + i, n - 1)
            j = lst[pos]
            mt = dot_nt(ub[pos], lvb[pos]).astype(BF16)
            mix[j] = mt
            hi, lo = split2(dot_nn(zeta(j), mt) * valid)
            res = dot_nn(jnp.concatenate([hi, lo], axis=0), lub[pos])
            acc[meta[M_T + j]] += res[:R] + res[R:]
        return carry

    lax.fori_loop(0, (n + 3) // 4, group, 0)

    def tile(m, carry):
        s = lst[N_LOW + m]
        pltpu.make_async_copy(nt.at[0], nb.at[m], nsems.at[0, m]).wait()
        pltpu.make_async_copy(lv.at[0], unb.at[m], nsems.at[1, m]).wait()
        left = dot_nt(unb[m], nb[m]).astype(BF16)
        lt[s] = left
        acc[meta[M_T + N_LOW + s]] += dot_nn(zeta(N_LOW + s), left)
        return carry

    lax.fori_loop(0, nn, tile, 0)


def pairs_a_kernel(meta, u0, u1, u3, z0, z1, z3, lv, lu, nt, acc, mix, lt, plan, zbuf, *scratch):
    def own(r):
        rel = r >> 3
        return ((rel == 0, u0, 0), (rel == 1, u1, 0), (rel == 3, u3, 0))

    acc[...] = jnp.zeros_like(acc)
    for n, ref in ((0, z0), (1, z1), (3, z3)):
        zbuf[n] = ref[...]
    pairs_body(meta, lambda rel: rel != 2, own, zbuf, lv, lu, nt, mix, lt, acc, *scratch)
    build_plan(meta, plan)


def pairs_b_kernel(meta, u2a, u2b, z2, acc_in, lv, lu, nt, keep, send, mix, lt, zbuf, acc, *scratch):
    def own(r):
        first = (r & 7) < PLUS_TILES
        return ((first, u2a, 0), (jnp.logical_not(first), u2b, PLUS_TILES))

    acc[...] = acc_in[...]
    zbuf[2] = z2[...]
    pairs_body(meta, lambda rel: rel == 2, own, zbuf, lv, lu, nt, mix, lt, acc, *scratch)
    core = meta[M_CORE]
    keep[...] = acc[pl.ds(core * 4, 4)]
    send[...] = acc[pl.ds(4 - core * 4, 4)]


ACC = jax.ShapeDtypeStruct((8, R, B), F32)
MIX = jax.ShapeDtypeStruct((N_LOW, R, R), BF16)
LEFT = jax.ShapeDtypeStruct((N_NEAR, R, B), BF16)
QUAD = jax.ShapeDtypeStruct((4, R, B), F32)
PAIR_SCRATCH = [
    pltpu.SMEM((N_PAIR,), jnp.int32),
    pltpu.VMEM((N_LOW, R, B), BF16),
    pltpu.VMEM((N_LOW, R, B), BF16),
    pltpu.VMEM((N_LOW, R, B), BF16),
    pltpu.VMEM((N_NEAR, B, B), BF16),
    pltpu.VMEM((N_NEAR, R, B), BF16),
    pltpu.SemaphoreType.DMA((3, N_LOW)),
    pltpu.SemaphoreType.DMA((2, N_NEAR)),
]
ZBUF = pltpu.VMEM((4, HALF, R, 128), BF16)


def pairs_a(meta, us, zs, low_v, low_u, near):
    return pl.pallas_call(
        pairs_a_kernel,
        out_shape=(ACC, MIX, LEFT, jax.ShapeDtypeStruct((128,), jnp.int32)),
        in_specs=[SMEM] + [ANY] * 3 + [VM] * 3 + [ANY] * 3,
        out_specs=(VM, VM, VM, SMEM),
        scratch_shapes=[ZBUF] + PAIR_SCRATCH,
        compiler_params=PARAMS,
        name="pairs_a",
    )(meta, *in_hbm(*us), *zs, *in_hbm(low_v, low_u, near))


def pairs_b(meta, us, z2, acc, low_v, low_u, near):
    return pl.pallas_call(
        pairs_b_kernel,
        out_shape=(QUAD, QUAD, MIX, LEFT),
        in_specs=[SMEM] + [ANY] * 2 + [VM, VM] + [ANY] * 3,
        out_specs=(VM,) * 4,
        scratch_shapes=[ZBUF, pltpu.VMEM((8, R, B), F32)] + PAIR_SCRATCH,
        compiler_params=PARAMS,
        name="pairs_b",
    )(meta, *in_hbm(*us), z2, acc, *in_hbm(low_v, low_u, near))


SLOTS = 56


def image_kernel(
    meta, plan, s0, s1, s2, s3, r0, r1, r2, r3, v0, v1, v2a, v2b, v3, lu, mixa, mixb, lta, ltb,
    keep, send, sall, lub, vb, nvb, acc, sems, nsems
):
    def own(r):
        rel = r >> 3
        low = (r & 7) < 4
        return (
            (rel == 0, v0, 0),
            (rel == 1, v1, 0),
            ((rel == 2) & low, v2a, 0),
            ((rel == 2) & jnp.logical_not(low), v2b, 4),
            (rel == 3, v3, 0),
        )

    count = plan[127]

    def load(i, carry):
        j = plan[i] & 255
        pltpu.make_async_copy(lu.at[j], lub.at[i], sems.at[0, i]).start()
        start_tile(meta[j], own, vb.at[i], sems.at[1, i])
        return carry

    lax.fori_loop(0, count, load, 0)
    live = meta[M_COUNT]

    def nload(s, carry):
        start_tile(meta[N_LOW + s], own, nvb.at[s], nsems.at[s])
        return carry

    lax.fori_loop(0, live, nload, 0)
    acc[...] = jnp.zeros_like(acc)
    core = meta[M_CORE]
    z = meta[M_Z]
    for n, ref in enumerate((s0, s1, s2, s3)):
        sall[core * 4 + ((z + n) & 3)] = ref[...]
    for n, ref in enumerate((r0, r1, r2, r3)):
        sall[(1 - core) * 4 + ((z + n) & 3)] = ref[...]

    def chunk(m, carry):
        at = m * 4
        for i in range(4):
            pltpu.make_async_copy(lu.at[0], lub.at[at + i], sems.at[0, at + i]).wait()
        t = plan[64 + m]
        q = dot_nt(lub[pl.ds(at, 4)].reshape(4 * R, B), sall[t])
        parts = []
        for i in range(4):
            e = plan[at + i]
            j = e & 255
            mt = jnp.where((meta[j] >> 3) == 2, mixb[j], mixa[j])
            hi, lo = split2(q[i * R : (i + 1) * R])
            both = dot_nn(mt, jnp.concatenate([hi, lo], axis=1))
            parts.append((both[:, :R] + both[:, R:]) * (e >> 8).astype(F32))
        p = jnp.concatenate(parts, axis=0).T
        hi, lo = split2(p)
        for i in range(4):
            pltpu.make_async_copy(lu.at[0], vb.at[at + i], sems.at[1, at + i]).wait()
        res = dot_nn(jnp.concatenate([hi, lo], axis=0), vb[pl.ds(at, 4)].reshape(4 * R, B))
        acc[t] += res[:R] + res[R:]
        return carry

    lax.fori_loop(0, count // 4, chunk, 0)

    def near(s, carry):
        t = meta[M_T + N_LOW + s]
        left = jnp.where((meta[N_LOW + s] >> 3) == 2, ltb[s], lta[s])
        hi, lo = split2(dot_nt(sall[t], left))
        pltpu.make_async_copy(lu.at[0], nvb.at[s], nsems.at[s]).wait()
        res = dot_nn(jnp.concatenate([hi, lo], axis=0), nvb[s])
        acc[t] += res[:R] + res[R:]
        return carry

    lax.fori_loop(0, live, near, 0)
    flip = acc[...].reshape(8 * R, B).T.reshape(16, 2, 32, 8 * R)
    first = core == 0
    keep[...] = jnp.where(first, flip[:, 0], flip[:, 1])
    send[...] = jnp.where(first, flip[:, 1], flip[:, 0])


def image_part(meta, plan, tiles, vs, low_u, mixes, lefts):
    half = jax.ShapeDtypeStruct((16, 32, 8 * R), F32)
    return pl.pallas_call(
        image_kernel,
        out_shape=(half, half, jax.ShapeDtypeStruct((8, R, B), BF16)),
        in_specs=[SMEM, SMEM] + [VM] * 8 + [ANY] * 6 + [VM] * 4,
        out_specs=(VM,) * 3,
        scratch_shapes=[
            pltpu.VMEM((SLOTS, R, B), BF16),
            pltpu.VMEM((SLOTS, R, B), BF16),
            pltpu.VMEM((N_NEAR, R, B), BF16),
            pltpu.VMEM((8, R, B), F32),
            pltpu.SemaphoreType.DMA((2, SLOTS)),
            pltpu.SemaphoreType.DMA((N_NEAR,)),
        ],
        compiler_params=PARAMS,
        name="image_part",
    )(meta, plan, *tiles, *in_hbm(*vs, low_u), *mixes, *lefts)


def dot_exact(a, b):
    return lax.dot_general(
        a, b, (((1,), (1,)), ((), ())), precision=lax.Precision.HIGHEST, preferred_element_type=F32
    )


def eliminate(m, ks):
    for k in ks:
        r0 = k // 8 * 8
        block = m[:, r0:, :]
        piv = m[:, k : k + 1, :]
        scaled = piv * (1.0 / piv[:, :, k : k + 1])
        fac = block[:, :, k : k + 1]
        if r0 + 8 > k:
            rows = lax.broadcasted_iota(jnp.int32, fac.shape, 1) + r0
            fac = jnp.where(rows > k, fac, 0.0)
        m[:, r0:, :] = block - fac * scaled


def factor_0_kernel(s_ref, m):
    lane = lax.broadcasted_iota(jnp.int32, (R, 2 * R), 1)
    row = lax.broadcasted_iota(jnp.int32, (R, 2 * R), 0)
    eye = (lane == row + R).astype(F32)
    for t in range(8):
        s = s_ref[t]
        g = dot_nt(s, s)
        m[t] = jnp.where(lane < R, jnp.concatenate([g, g], axis=1), eye)
    eliminate(m, range(CUT0))


def factor_1_kernel(m_in, m):
    m[...] = m_in[...]
    eliminate(m, range(CUT0, CUT1))


def factor_2_kernel(meta, s_ref, m_in, basis, inv, m):
    m[...] = m_in[...]
    eliminate(m, range(CUT1, R))
    lane = lax.broadcasted_iota(jnp.int32, (R, 2 * R), 1)
    row = lax.broadcasted_iota(jnp.int32, (R, 2 * R), 0)
    pick_row = lax.broadcasted_iota(jnp.int32, (32, B), 0) + meta[M_S] * 32
    pick = (lax.broadcasted_iota(jnp.int32, (32, B), 1) == pick_row).astype(BF16)
    for t in range(8):
        a = m[t]
        diag = jnp.sum(jnp.where(lane == row, a, 0.0), axis=1, keepdims=True)
        li = a[:, R:] * lax.rsqrt(diag)
        inv[t] = li
        basis[t] = 32.0 * dot_exact(dot_nt(pick, s_ref[t]), li)


CUT0 = 6
CUT1 = 36
STATE = jax.ShapeDtypeStruct((8, R, 2 * R), F32)


def factor(meta, s):
    m = pl.pallas_call(
        factor_0_kernel, out_shape=STATE, in_specs=[VM], out_specs=VM, compiler_params=SMALL, name="factor_0"
    )(s)
    m = pl.pallas_call(
        factor_1_kernel, out_shape=STATE, in_specs=[VM], out_specs=VM, compiler_params=SMALL, name="factor_1"
    )(m)
    return pl.pallas_call(
        factor_2_kernel,
        out_shape=(jax.ShapeDtypeStruct((8, 32, R), F32), jax.ShapeDtypeStruct((8, R, R), F32)),
        in_specs=[SMEM, VM, VM],
        out_specs=(VM, VM),
        scratch_shapes=[pltpu.VMEM((8, R, 2 * R), F32)],
        compiler_params=SMALL,
        name="factor_2",
    )(meta, s, m)


def first_sum(meta, a, b):
    part = (a.shape[0] // 4,) + a.shape[1:]
    n = part[0]

    def body(meta, a, b, own, p1, p2, p3):
        z = meta[M_Z]
        for k, out in enumerate((own, p1, p2, p3)):
            at = pl.ds(((z + k) & 3) * n, n)
            out[...] = (a[at] + b[at]).astype(out.dtype)

    outs = pl.pallas_call(
        body,
        out_shape=(jax.ShapeDtypeStruct(part, F32),) + (jax.ShapeDtypeStruct(part, BF16),) * 3,
        in_specs=[SMEM, VM, VM],
        out_specs=(VM,) * 4,
        compiler_params=SMALL,
        name="first_sum",
    )(meta, a, b)
    return outs


def add4(a, b, c, d, dtype):
    def body(a, b, c, d, out):
        out[...] = (a[...].astype(F32) + b[...].astype(F32) + c[...].astype(F32) + d[...].astype(F32)).astype(dtype)

    return pl.pallas_call(
        body,
        out_shape=jax.ShapeDtypeStruct(a.shape, dtype),
        in_specs=[VM] * 4,
        out_specs=VM,
        compiler_params=SMALL,
        name="add4",
    )(a, b, c, d)


def second_sum(meta, a, b, c, d):
    shape = a.shape[1:]

    def body(meta, a, b, c, d, own, p1, p2, p3):
        y = meta[M_Y]
        for k, out in enumerate((own, p1, p2, p3)):
            at = (y + k) & 3
            out[...] = a[at] + b[at].astype(F32) + c[at].astype(F32) + d[at].astype(F32)

    return pl.pallas_call(
        body,
        out_shape=(jax.ShapeDtypeStruct(shape, F32),) * 4,
        in_specs=[SMEM] + [VM] * 4,
        out_specs=(VM,) * 4,
        compiler_params=SMALL,
        name="second_sum",
    )(meta, a, b, c, d)


def finish(inv, a, b, c, d):
    def body(inv, a, b, c, d, out):
        total = a[...] + b[...] + c[...] + d[...]
        for t in range(8):
            out[t] = dot_exact(total[:, t * R : (t + 1) * R], inv[t])

    return pl.pallas_call(
        body,
        out_shape=jax.ShapeDtypeStruct((8, 32, R), F32),
        in_specs=[VM] * 5,
        out_specs=VM,
        compiler_params=SMALL,
        name="finish",
    )(inv, a, b, c, d)


def along_x(x, step):
    return lax.ppermute(x, "tgt", [(i, (i + step) % 4) for i in range(4)])


def along_inner(x, dz=0, dy=0, dc=0):
    pairs = []
    for z in range(4):
        for y in range(4):
            for c in range(2):
                to = (((z + dz) % 4) * 4 + (y + dy) % 4) * 2 + (c ^ dc)
                pairs.append(((z * 4 + y) * 2 + c, to))
    return lax.ppermute(x, "inner", pairs)


def after(x, *others):
    return lax.optimization_barrier((x,) + others)[0]


def steps(
    near_tiles, near_target, near_right, near_count, low_u, low_v, low_target, low_right, right_u, right_v, probe_seed
):
    g = lax.axis_index("tgt")
    s = lax.axis_index("inner")
    rights = jnp.concatenate([low_right, near_right])
    targets = jnp.concatenate([low_target, near_target])
    req = jnp.concatenate([rights, targets, probe_seed, jnp.zeros((128 - 2 * N_PAIR - 8,), jnp.int32)])[None]
    place = jnp.stack([near_count[0], s & 1, s >> 3, (s >> 1) & 3, s]).astype(jnp.int32)
    meta = jnp.concatenate(
        [(rights - 8 * g) & 31, targets, place, jnp.zeros((128 - 2 * N_PAIR - 5,), jnp.int32)]
    )

    u3 = along_x(right_u, 1)
    u1 = along_x(right_u, 3)
    reqs = jnp.concatenate([req, along_x(req, 3), along_x(req, 2), along_x(req, 1)])
    o0, o1, o2, o3 = zeta_home(after(reqs, meta), right_v)
    z1 = along_x(o3, 3)
    z3 = along_x(o1, 1)
    z2 = along_x(o2, 2)
    u2a = along_x(u3[:PLUS_TILES], 1)
    u2b = along_x(u1[PLUS_TILES:], 3)
    v3 = along_x(right_v, 1)
    v1 = along_x(right_v, 3)

    acc, mixa, lta, plan = pairs_a(meta, (right_u, u1, u3), (o0, z1, z3), low_v, low_u, near_tiles)
    keep, send, mixb, ltb = pairs_b(meta, (u2a, u2b), z2, acc, low_v, low_u, near_tiles)

    other = along_inner(send, dc=1)
    own, p1, p2, p3 = first_sum(meta, keep, other)
    col = add4(
        own[0], along_inner(p1[0], dz=1), along_inner(p2[0], dz=2), along_inner(p3[0], dz=3), BF16
    )
    v2a = along_x(v3[:4], 1)
    v2b = along_x(v1[4:], 3)
    tile = add4(col, along_inner(col, dy=1), along_inner(col, dy=2), along_inner(col, dy=3), BF16)
    mine = (tile, along_inner(tile, dz=3), along_inner(tile, dz=2), along_inner(tile, dz=1))
    theirs = tuple(along_inner(x, dc=1) for x in mine)

    ikeep, isend, sall = image_part(
        meta, plan, mine + theirs, (right_v, v1, v2a, v2b, v3), low_u, (mixa, mixb), (lta, ltb)
    )
    basis, inv = factor(meta, sall)

    iother = along_inner(isend, dc=1)
    own, p1, p2, p3 = first_sum(meta, ikeep, iother)
    own, p1, p2, p3 = second_sum(
        meta, own, along_inner(p1, dz=1), along_inner(p2, dz=2), along_inner(p3, dz=3)
    )
    image = finish(inv, own, along_inner(p1, dy=1), along_inner(p2, dy=2), along_inner(p3, dy=3))
    return (jnp.swapaxes(basis, 1, 2), jnp.swapaxes(image, 1, 2))


def solution(mesh):
    dev = P(("tgt", "inner"))
    return jax.shard_map(
        steps,
        mesh=mesh,
        in_specs=(dev,) * 10 + (P("tgt"),),
        out_specs=(P("tgt", None, "inner"), P("tgt", None, "inner")),
        check_vma=False,
    )
```

```python
import jax
import jax.numpy as jnp
from jax import lax
from jax.experimental import pallas as pl
from jax.experimental.pallas import tpu as pltpu
from jax.sharding import PartitionSpec as P


B = 1024
R = 64
MOD = 65521
N_LOW = 32
N_NEAR = 4
N_PAIR = N_LOW + N_NEAR
HALF = N_PAIR // 2
F32 = jnp.float32
BF16 = jnp.bfloat16


M_T = N_PAIR
M_COUNT = 2 * N_PAIR
M_CORE = M_COUNT + 1
M_Z = M_COUNT + 2
M_Y = M_COUNT + 3
M_S = M_COUNT + 4

SMEM = pl.BlockSpec(memory_space=pltpu.MemorySpace.SMEM)
VM = pl.BlockSpec(memory_space=pltpu.MemorySpace.VMEM)
ANY = pl.BlockSpec(memory_space=pltpu.MemorySpace.HBM)
PARAMS = pltpu.CompilerParams(vmem_limit_bytes=32 * 1024 * 1024)
SMALL = pltpu.CompilerParams(vmem_limit_bytes=12 * 1024 * 1024)


def in_hbm(*xs):
    return tuple(pltpu.with_memory_space_constraint(x, pltpu.MemorySpace.HBM) for x in xs)


def dot_nt(a, b):
    return lax.dot_general(a, b, (((1,), (1,)), ((), ())), preferred_element_type=F32)


def dot_nn(a, b):
    return lax.dot_general(a, b, (((1,), (0,)), ((), ())), preferred_element_type=F32)


def split2(x):
    hi = x.astype(BF16)
    return hi, (x - hi.astype(F32)).astype(BF16)


def zeta_kernel(req, v_ref, o0, o1, o2, o3, base, probe, tab):
    c = lax.broadcasted_iota(jnp.int32, (R, B), 0)
    i = lax.broadcasted_iota(jnp.int32, (R, B), 1)
    f = i * i * 7 + i * c * 131 + c * c * 17 + i * 7919 + c * 104729
    q = (f.astype(F32) * (1.0 / MOD)).astype(jnp.int32)
    f = f - q * MOD
    f = jnp.where(f < 0, f + MOD, f)
    f = jnp.where(f >= MOD, f - MOD, f)
    base[...] = f.astype(F32)
    v = v_ref[...].reshape(8 * R, B)
    left = lax.broadcasted_iota(jnp.int32, (4 * R, 128), 1) < R

    def batch(b, carry):
        row = b // 2
        for u in range(4):
            seed = req[row, 2 * N_PAIR + (b % 2) * 4 + u]
            shift = lax.rem(seed * 9973, MOD).astype(F32)
            code = base[...] + shift
            code = jnp.where(code >= MOD, code - MOD, code)
            probe[u * R : (u + 1) * R] = ((code - 32760.0) * (1.0 / 32768.0)).astype(BF16)
        res = dot_nt(probe[...], v)
        for ip in range(4):
            blk = res[:, ip * 128 : (ip + 1) * 128]
            rolled = pltpu.roll(blk, R, 1)
            even = jnp.where(left, blk, rolled)
            odd = jnp.where(left, rolled, blk)
            for u in range(4):
                tab[b * 4 + u, 2 * ip] = even[u * R : (u + 1) * R]
                tab[b * 4 + u, 2 * ip + 1] = odd[u * R : (u + 1) * R]
        return carry

    lax.fori_loop(0, 8, batch, 0)
    lm = lax.broadcasted_iota(jnp.int32, (R, 128), 1) < R

    def slot(p, carry):
        for q, out in enumerate((o0, o1, o2, o3)):
            ra = req[q, p] & 7
            ta = req[q, N_PAIR + p]
            rb = req[q, HALF + p] & 7
            tb = req[q, N_PAIR + HALF + p]
            out[p] = jnp.where(lm, tab[q * 8 + ta, ra], tab[q * 8 + tb, rb]).astype(BF16)
        return carry

    lax.fori_loop(0, HALF, slot, 0)


def zeta_home(req, v_own):
    out = jax.ShapeDtypeStruct((HALF, R, 128), BF16)
    return pl.pallas_call(
        zeta_kernel,
        out_shape=(out,) * 4,
        in_specs=[SMEM, VM],
        out_specs=(VM,) * 4,
        scratch_shapes=[
            pltpu.VMEM((R, B), F32),
            pltpu.VMEM((4 * R, B), BF16),
            pltpu.VMEM((32, 8, R, 128), F32),
        ],
        compiler_params=PARAMS,
        name="zeta_home",
    )(req, v_own)


PLUS_TILES = 4


def start_tile(r, own, dst, sem):
    for cond, ref, shift in own(r):

        @pl.when(cond)
        def _():
            pltpu.make_async_copy(ref.at[(r & 7) - shift], dst, sem).start()


def plan_kernel(meta, plan, count, place):
    for t in range(8):
        count[t] = 0

    def tally(j, carry):
        t = meta[M_T + j]
        count[t] = count[t] + 1
        return carry

    lax.fori_loop(0, N_LOW, tally, 0)

    def start(t, slot):
        place[t] = slot
        full = (count[t] + 3) // 4

        def mark(c, carry):
            plan[64 + slot // 4 + c] = t
            return carry

        lax.fori_loop(0, full, mark, 0)
        return slot + full * 4

    plan[127] = lax.fori_loop(0, 8, start, 0)

    def put(j, carry):
        t = meta[M_T + j]
        at = place[t]
        plan[at] = j + 256
        place[t] = at + 1
        return carry

    lax.fori_loop(0, N_LOW, put, 0)

    def pad(t, carry):
        end = place[t]

        def fill(i, carry):
            plan[i] = plan[end - 1] & 255
            return carry

        return lax.fori_loop(end, (end + 3) // 4 * 4, fill, carry)

    lax.fori_loop(0, 8, pad, 0)


def make_plan(meta):
    return pl.pallas_call(
        plan_kernel,
        out_shape=jax.ShapeDtypeStruct((128,), jnp.int32),
        in_specs=[SMEM],
        out_specs=SMEM,
        scratch_shapes=[pltpu.SMEM((8,), jnp.int32), pltpu.SMEM((8,), jnp.int32)],
        compiler_params=SMALL,
        name="make_plan",
    )(meta)


def left_body(meta, mine, own, lv, nt, mix, lt, lst, lvb, ub, nb, unb, sems, nsems):
    def low(j, n):
        r = meta[j]
        hit = mine(r >> 3)

        @pl.when(hit)
        def _():
            lst[n] = j
            pltpu.make_async_copy(lv.at[j], lvb.at[n], sems.at[0, n]).start()
            start_tile(r, own, ub.at[n], sems.at[1, n])

        return n + hit.astype(jnp.int32)

    n = lax.fori_loop(0, N_LOW, low, 0)

    def near(s, m):
        r = meta[N_LOW + s]
        hit = mine(r >> 3) & (s < meta[M_COUNT])

        @pl.when(hit)
        def _():
            lst[N_LOW + m] = s
            pltpu.make_async_copy(nt.at[s], nb.at[m], nsems.at[0, m]).start()
            start_tile(r, own, unb.at[m], nsems.at[1, m])

        return m + hit.astype(jnp.int32)

    nn = lax.fori_loop(0, N_NEAR, near, 0)

    def group(g, carry):
        for i in range(4):
            pos = g * 4 + i

            @pl.when(pos < n)
            def _():
                pltpu.make_async_copy(lv.at[0], lvb.at[pos], sems.at[0, pos]).wait()
                pltpu.make_async_copy(lv.at[0], ub.at[pos], sems.at[1, pos]).wait()

        spots = [jnp.minimum(g * 4 + i, n - 1) for i in range(4)]
        done = [dot_nt(ub[pos], lvb[pos]).astype(BF16) for pos in spots]
        for pos, mt in zip(spots, done):
            mix[lst[pos]] = mt
        return carry

    lax.fori_loop(0, (n + 3) // 4, group, 0)

    def tile(m, carry):
        pltpu.make_async_copy(nt.at[0], nb.at[m], nsems.at[0, m]).wait()
        pltpu.make_async_copy(lv.at[0], unb.at[m], nsems.at[1, m]).wait()
        lt[lst[N_LOW + m]] = dot_nt(unb[m], nb[m]).astype(BF16)
        return carry

    lax.fori_loop(0, nn, tile, 0)


def sum_body(meta, mine, zbuf, lu, mix, lt, acc, lst, lub, sems):
    def low(j, n):
        hit = mine(meta[j] >> 3)

        @pl.when(hit)
        def _():
            lst[n] = j
            pltpu.make_async_copy(lu.at[j], lub.at[n], sems.at[n]).start()

        return n + hit.astype(jnp.int32)

    n = lax.fori_loop(0, N_LOW, low, 0)

    def zeta(j):
        second = j >= HALF
        blk = zbuf[meta[j] >> 3, jnp.where(second, j - HALF, j)].astype(F32)
        return jnp.where(second, pltpu.roll(blk, R, 1), blk)[:, :R].astype(BF16)

    def tile(s, carry):
        @pl.when(mine(meta[N_LOW + s] >> 3))
        def _():
            acc[meta[M_T + N_LOW + s]] += dot_nn(zeta(N_LOW + s), lt[s])

        return carry

    lax.fori_loop(0, meta[M_COUNT], tile, 0)

    def group(g, carry):
        terms = []
        for i in range(4):
            pos = jnp.minimum(g * 4 + i, n - 1)
            j = lst[pos]
            hi, lo = split2(dot_nn(zeta(j), mix[j]) * (g * 4 + i < n).astype(F32))
            terms.append((pos, j, jnp.concatenate([hi, lo], axis=0)))
        for i in range(4):
            pos = g * 4 + i

            @pl.when(pos < n)
            def _():
                pltpu.make_async_copy(lu.at[0], lub.at[pos], sems.at[pos]).wait()

        for pos, j, w in terms:
            res = dot_nn(w, lub[pos])
            acc[meta[M_T + j]] += res[:R] + res[R:]
        return carry

    lax.fori_loop(0, (n + 3) // 4, group, 0)


N_LEFT = 7


def pairs_0_kernel(meta, u0, z0, lv, lu, nt, acc, mix, lt, zbuf, *scratch):
    acc[...] = jnp.zeros_like(acc)
    zbuf[0] = z0[...]
    mine = lambda rel: rel == 0
    left_body(meta, mine, lambda r: ((r >= 0, u0, 0),), lv, nt, mix, lt, *scratch[:N_LEFT])
    sum_body(meta, mine, zbuf, lu, mix, lt, acc, *scratch[N_LEFT:])


def near_side(rel):
    return (rel == 1) | (rel == 3)


def far_side(rel):
    return rel == 2


def left_a_kernel(meta, u1, u3, mix_in, lt_in, lv, nt, mix, lt, *scratch):
    mix[...] = mix_in[...]
    lt[...] = lt_in[...]
    left_body(
        meta, near_side, lambda r: ((r < 16, u1, 0), (r >= 16, u3, 0)), lv, nt, mix, lt, *scratch
    )


def left_b_kernel(meta, u2a, u2b, mix_in, lt_in, lv, nt, mix, lt, *scratch):
    def own(r):
        first = (r & 7) < PLUS_TILES
        return ((first, u2a, 0), (jnp.logical_not(first), u2b, PLUS_TILES))

    mix[...] = mix_in[...]
    lt[...] = lt_in[...]
    left_body(meta, far_side, own, lv, nt, mix, lt, *scratch)


def sum_a_kernel(meta, z1, z3, acc_in, mix, lt, lu, acc, zbuf, *scratch):
    acc[...] = acc_in[...]
    zbuf[1] = z1[...]
    zbuf[3] = z3[...]
    sum_body(meta, near_side, zbuf, lu, mix, lt, acc, *scratch)


def sum_b_kernel(meta, z2, acc_in, mix, lt, lu, keep, send, zbuf, acc, *scratch):
    acc[...] = acc_in[...]
    zbuf[2] = z2[...]
    sum_body(meta, far_side, zbuf, lu, mix, lt, acc, *scratch)
    core = meta[M_CORE]
    keep[...] = acc[pl.ds(core * 4, 4)]
    send[...] = acc[pl.ds(4 - core * 4, 4)]


ACC = jax.ShapeDtypeStruct((8, R, B), F32)
MIX = jax.ShapeDtypeStruct((N_LOW, R, R), BF16)
LEFT = jax.ShapeDtypeStruct((N_NEAR, R, B), BF16)
QUAD = jax.ShapeDtypeStruct((4, R, B), F32)
LEFT_SCRATCH = [
    pltpu.SMEM((N_PAIR,), jnp.int32),
    pltpu.VMEM((N_LOW, R, B), BF16),
    pltpu.VMEM((N_LOW, R, B), BF16),
    pltpu.VMEM((N_NEAR, B, B), BF16),
    pltpu.VMEM((N_NEAR, R, B), BF16),
    pltpu.SemaphoreType.DMA((2, N_LOW)),
    pltpu.SemaphoreType.DMA((2, N_NEAR)),
]
SUM_SCRATCH = [
    pltpu.SMEM((N_LOW,), jnp.int32),
    pltpu.VMEM((N_LOW, R, B), BF16),
    pltpu.SemaphoreType.DMA((N_LOW,)),
]
ZBUF = pltpu.VMEM((4, HALF, R, 128), BF16)


def pairs_0(meta, u0, z0, low_v, low_u, near):
    return pl.pallas_call(
        pairs_0_kernel,
        out_shape=(ACC, MIX, LEFT),
        in_specs=[SMEM, ANY, VM] + [ANY] * 3,
        out_specs=(VM, VM, VM),
        scratch_shapes=[ZBUF] + LEFT_SCRATCH + SUM_SCRATCH,
        compiler_params=PARAMS,
        name="pairs_0",
    )(meta, *in_hbm(u0), z0, *in_hbm(low_v, low_u, near))


def left_part(kernel, meta, us, mix, lt, low_v, near):
    return pl.pallas_call(
        kernel,
        out_shape=(MIX, LEFT),
        in_specs=[SMEM] + [ANY] * 2 + [VM] * 2 + [ANY] * 2,
        out_specs=(VM, VM),
        scratch_shapes=LEFT_SCRATCH,
        compiler_params=PARAMS,
    )(meta, *in_hbm(*us), mix, lt, *in_hbm(low_v, near))


def sum_a(meta, z1, z3, acc, mix, lt, low_u):
    return pl.pallas_call(
        sum_a_kernel,
        out_shape=ACC,
        in_specs=[SMEM] + [VM] * 5 + [ANY],
        out_specs=VM,
        scratch_shapes=[ZBUF] + SUM_SCRATCH,
        compiler_params=PARAMS,
        name="sum_a",
    )(meta, z1, z3, acc, mix, lt, *in_hbm(low_u))


def sum_b(meta, z2, acc, mix, lt, low_u):
    return pl.pallas_call(
        sum_b_kernel,
        out_shape=(QUAD, QUAD),
        in_specs=[SMEM] + [VM] * 4 + [ANY],
        out_specs=(VM, VM),
        scratch_shapes=[ZBUF, pltpu.VMEM((8, R, B), F32)] + SUM_SCRATCH,
        compiler_params=PARAMS,
        name="sum_b",
    )(meta, z2, acc, mix, lt, *in_hbm(low_u))


SLOTS = 56


def proj_kernel(
    meta, plan, s0, s1, s2, s3, r0, r1, r2, r3, lu, mix, lt, p_ref, pn_ref, sall, lub, sems
):
    count = plan[127]

    def load(i, carry):
        pltpu.make_async_copy(lu.at[plan[i] & 255], lub.at[i], sems.at[i]).start()
        return carry

    lax.fori_loop(0, count, load, 0)
    core = meta[M_CORE]
    z = meta[M_Z]
    for n, ref in enumerate((s0, s1, s2, s3)):
        sall[core * 4 + ((z + n) & 3)] = ref[...]
    for n, ref in enumerate((r0, r1, r2, r3)):
        sall[(1 - core) * 4 + ((z + n) & 3)] = ref[...]

    for s in range(N_NEAR):
        hi, lo = split2(dot_nt(sall[meta[M_T + N_LOW + s]], lt[s]))
        pn_ref[s] = jnp.concatenate([hi, lo], axis=0)
    n = count // 4

    def ready(m):
        @pl.when(m < n)
        def _():
            for i in range(4):
                at = m * 4 + i
                pltpu.make_async_copy(lu.at[0], lub.at[at], sems.at[at]).wait()

    def chunk(m):
        at = m * 4
        q = dot_nt(lub[pl.ds(at, 4)].reshape(4 * R, B), sall[plan[64 + m]])
        parts = []
        for i in range(4):
            e = plan[at + i]
            hi, lo = split2(q[i * R : (i + 1) * R])
            both = dot_nn(mix[e & 255], jnp.concatenate([hi, lo], axis=1))
            parts.append((both[:, :R] + both[:, R:]) * (e >> 8).astype(F32))
        hi, lo = split2(jnp.concatenate(parts, axis=0).T)
        return jnp.concatenate([hi, lo], axis=0)

    def two(i, carry):
        m0 = 2 * i
        m1 = jnp.minimum(m0 + 1, n - 1)
        ready(m0)
        ready(m0 + 1)
        p0 = chunk(m0)
        p1 = chunk(m1)
        p_ref[m0] = p0
        p_ref[m1] = p1
        return carry

    lax.fori_loop(0, (n + 1) // 2, two, 0)


def image_kernel(meta, plan, p_ref, pn_ref, v0, v1, v2a, v2b, v3, keep, send, vb, nvb, acc, sems, nsems):
    def own(r):
        rel = r >> 3
        low = (r & 7) < 4
        return (
            (rel == 0, v0, 0),
            (rel == 1, v1, 0),
            ((rel == 2) & low, v2a, 0),
            ((rel == 2) & jnp.logical_not(low), v2b, 4),
            (rel == 3, v3, 0),
        )

    count = plan[127]

    def load(i, carry):
        start_tile(meta[plan[i] & 255], own, vb.at[i], sems.at[i])
        return carry

    lax.fori_loop(0, count, load, 0)

    def nload(s, carry):
        start_tile(meta[N_LOW + s], own, nvb.at[s], nsems.at[s])
        return carry

    lax.fori_loop(0, meta[M_COUNT], nload, 0)
    acc[...] = jnp.zeros_like(acc)

    def chunk(m, carry):
        at = m * 4
        for i in range(4):
            pltpu.make_async_copy(v0.at[0], vb.at[at + i], sems.at[at + i]).wait()
        res = dot_nn(p_ref[m], vb[pl.ds(at, 4)].reshape(4 * R, B))
        acc[plan[64 + m]] += res[:R] + res[R:]
        return carry

    lax.fori_loop(0, count // 4, chunk, 0)

    def near(s, carry):
        pltpu.make_async_copy(v0.at[0], nvb.at[s], nsems.at[s]).wait()
        res = dot_nn(pn_ref[s], nvb[s])
        acc[meta[M_T + N_LOW + s]] += res[:R] + res[R:]
        return carry

    lax.fori_loop(0, meta[M_COUNT], near, 0)
    flip = acc[...].reshape(8 * R, B).T.reshape(16, 2, 32, 8 * R)
    first = meta[M_CORE] == 0
    keep[...] = jnp.where(first, flip[:, 0], flip[:, 1])
    send[...] = jnp.where(first, flip[:, 1], flip[:, 0])


def proj_part(meta, plan, tiles, low_u, mix, lt):
    return pl.pallas_call(
        proj_kernel,
        out_shape=(
            jax.ShapeDtypeStruct((SLOTS // 4, 2 * R, 4 * R), BF16),
            jax.ShapeDtypeStruct((N_NEAR, 2 * R, R), BF16),
            jax.ShapeDtypeStruct((8, R, B), BF16),
        ),
        in_specs=[SMEM, SMEM] + [VM] * 8 + [ANY] + [VM] * 2,
        out_specs=(VM,) * 3,
        scratch_shapes=[pltpu.VMEM((SLOTS, R, B), BF16), pltpu.SemaphoreType.DMA((SLOTS,))],
        compiler_params=PARAMS,
        name="proj_part",
    )(meta, plan, *tiles, *in_hbm(low_u), mix, lt)


def image_part(meta, plan, p, pn, vs):
    half = jax.ShapeDtypeStruct((16, 32, 8 * R), F32)
    return pl.pallas_call(
        image_kernel,
        out_shape=(half, half),
        in_specs=[SMEM, SMEM, VM, VM] + [ANY] * 5,
        out_specs=(VM,) * 2,
        scratch_shapes=[
            pltpu.VMEM((SLOTS, R, B), BF16),
            pltpu.VMEM((N_NEAR, R, B), BF16),
            pltpu.VMEM((8, R, B), F32),
            pltpu.SemaphoreType.DMA((SLOTS,)),
            pltpu.SemaphoreType.DMA((N_NEAR,)),
        ],
        compiler_params=PARAMS,
        name="image_part",
    )(meta, plan, p, pn, *in_hbm(*vs))


def dot_exact(a, b):
    return lax.dot_general(
        a, b, (((1,), (1,)), ((), ())), precision=lax.Precision.HIGHEST, preferred_element_type=F32
    )


def eliminate(m, ks):
    for k in ks:
        r0 = k // 8 * 8
        block = m[:, r0:, :]
        piv = m[:, k : k + 1, :]
        scaled = piv * (1.0 / piv[:, :, k : k + 1])
        fac = block[:, :, k : k + 1]
        if r0 + 8 > k:
            rows = lax.broadcasted_iota(jnp.int32, fac.shape, 1) + r0
            fac = jnp.where(rows > k, fac, 0.0)
        m[:, r0:, :] = block - fac * scaled


def factor_0_kernel(meta, s_ref, m, cols):
    lane = lax.broadcasted_iota(jnp.int32, (R, 2 * R), 1)
    row = lax.broadcasted_iota(jnp.int32, (R, 2 * R), 0)
    eye = (lane == row + R).astype(F32)
    pick_row = lax.broadcasted_iota(jnp.int32, (32, B), 0) + meta[M_S] * 32
    pick = (lax.broadcasted_iota(jnp.int32, (32, B), 1) == pick_row).astype(BF16)
    for t in range(8):
        s = s_ref[t]
        g = dot_nt(jnp.concatenate([s, pick], axis=0), s)
        m[t] = jnp.where(lane < R, jnp.concatenate([g[:R], g[:R]], axis=1), eye)
        cols[t] = g[R:]
    eliminate(m, range(CUT0))


def factor_1_kernel(m_in, m):
    m[...] = m_in[...]
    eliminate(m, range(CUT0, CUT1))


def factor_2_kernel(m_in, cols, basis, inv, m):
    m[...] = m_in[...]
    eliminate(m, range(CUT1, R))
    lane = lax.broadcasted_iota(jnp.int32, (R, 2 * R), 1)
    row = lax.broadcasted_iota(jnp.int32, (R, 2 * R), 0)
    for t in range(8):
        a = m[t]
        diag = jnp.sum(jnp.where(lane == row, a, 0.0), axis=1, keepdims=True)
        li = a[:, R:] * lax.rsqrt(diag)
        inv[t] = li
        basis[t] = 32.0 * dot_exact(cols[t], li)


CUT0 = 8
CUT1 = 48
STATE = jax.ShapeDtypeStruct((8, R, 2 * R), F32)
COLS = jax.ShapeDtypeStruct((8, 32, R), F32)


def factor(meta, s):
    m, cols = pl.pallas_call(
        factor_0_kernel,
        out_shape=(STATE, COLS),
        in_specs=[SMEM, VM],
        out_specs=(VM, VM),
        compiler_params=SMALL,
        name="factor_0",
    )(meta, s)
    m = pl.pallas_call(
        factor_1_kernel, out_shape=STATE, in_specs=[VM], out_specs=VM, compiler_params=SMALL, name="factor_1"
    )(m)
    return pl.pallas_call(
        factor_2_kernel,
        out_shape=(COLS, jax.ShapeDtypeStruct((8, R, R), F32)),
        in_specs=[VM, VM],
        out_specs=(VM, VM),
        scratch_shapes=[pltpu.VMEM((8, R, 2 * R), F32)],
        compiler_params=SMALL,
        name="factor_2",
    )(m, cols)


def first_sum(meta, a, b):
    part = (a.shape[0] // 4,) + a.shape[1:]
    n = part[0]

    def body(meta, a, b, own, p1, p2, p3):
        z = meta[M_Z]
        for k, out in enumerate((own, p1, p2, p3)):
            at = pl.ds(((z + k) & 3) * n, n)
            out[...] = (a[at] + b[at]).astype(out.dtype)

    outs = pl.pallas_call(
        body,
        out_shape=(jax.ShapeDtypeStruct(part, F32),) + (jax.ShapeDtypeStruct(part, BF16),) * 3,
        in_specs=[SMEM, VM, VM],
        out_specs=(VM,) * 4,
        compiler_params=SMALL,
        name="first_sum",
    )(meta, a, b)
    return outs


def add4(a, b, c, d, dtype):
    def body(a, b, c, d, out):
        out[...] = (a[...].astype(F32) + b[...].astype(F32) + c[...].astype(F32) + d[...].astype(F32)).astype(dtype)

    return pl.pallas_call(
        body,
        out_shape=jax.ShapeDtypeStruct(a.shape, dtype),
        in_specs=[VM] * 4,
        out_specs=VM,
        compiler_params=SMALL,
    )(a, b, c, d)


def second_sum(meta, a, b, c, d):
    shape = a.shape[1:]

    def body(meta, a, b, c, d, own, p1, p2, p3):
        y = meta[M_Y]
        for k, out in enumerate((own, p1, p2, p3)):
            at = (y + k) & 3
            out[...] = a[at] + b[at].astype(F32) + c[at].astype(F32) + d[at].astype(F32)

    return pl.pallas_call(
        body,
        out_shape=(jax.ShapeDtypeStruct(shape, F32),) * 4,
        in_specs=[SMEM] + [VM] * 4,
        out_specs=(VM,) * 4,
        compiler_params=SMALL,
        name="second_sum",
    )(meta, a, b, c, d)


def finish(inv, a, b, c, d):
    def body(inv, a, b, c, d, out):
        total = a[...] + b[...] + c[...] + d[...]
        for t in range(8):
            out[t] = dot_exact(total[:, t * R : (t + 1) * R], inv[t])

    return pl.pallas_call(
        body,
        out_shape=jax.ShapeDtypeStruct((8, 32, R), F32),
        in_specs=[VM] * 5,
        out_specs=VM,
        compiler_params=SMALL,
        name="finish",
    )(inv, a, b, c, d)


def along_x(x, step):
    return lax.ppermute(x, "tgt", [(i, (i + step) % 4) for i in range(4)])


def along_inner(x, dz=0, dy=0, dc=0):
    pairs = []
    for z in range(4):
        for y in range(4):
            for c in range(2):
                to = (((z + dz) % 4) * 4 + (y + dy) % 4) * 2 + (c ^ dc)
                pairs.append(((z * 4 + y) * 2 + c, to))
    return lax.ppermute(x, "inner", pairs)


def after(x, *others):
    return lax.optimization_barrier((x,) + others)[0]


def steps(
    near_tiles, near_target, near_right, near_count, low_u, low_v, low_target, low_right, right_u, right_v, probe_seed
):
    g = lax.axis_index("tgt")
    s = lax.axis_index("inner")
    rights = jnp.concatenate([low_right, near_right])
    targets = jnp.concatenate([low_target, near_target])
    req = jnp.concatenate([rights, targets, probe_seed, jnp.zeros((128 - 2 * N_PAIR - 8,), jnp.int32)])[None]
    place = jnp.stack([near_count[0], s & 1, s >> 3, (s >> 1) & 3, s]).astype(jnp.int32)
    meta = jnp.concatenate(
        [(rights - 8 * g) & 31, targets, place, jnp.zeros((128 - 2 * N_PAIR - 5,), jnp.int32)]
    )

    u3 = along_x(right_u, 1)
    u1 = along_x(right_u, 3)
    reqs = jnp.concatenate([req, along_x(req, 3), along_x(req, 2), along_x(req, 1)])
    o0, o1, o2, o3 = zeta_home(after(reqs, meta), right_v)
    z1 = along_x(o3, 3)
    z3 = along_x(o1, 1)
    z2 = along_x(o2, 2)
    u2a = along_x(u3[:PLUS_TILES], 1)
    u2b = along_x(u1[PLUS_TILES:], 3)
    v3 = along_x(right_v, 1)
    v1 = along_x(right_v, 3)

    acc, mix, lt = pairs_0(meta, right_u, o0, low_v, low_u, near_tiles)
    mix, lt = left_part(left_a_kernel, meta, (u1, u3), mix, lt, low_v, near_tiles)
    acc = sum_a(meta, z1, z3, acc, mix, lt, low_u)
    mix, lt = left_part(left_b_kernel, meta, (u2a, u2b), mix, lt, low_v, near_tiles)
    keep, send = sum_b(meta, z2, acc, mix, lt, low_u)

    plan = make_plan(after(meta, keep))

    other = along_inner(send, dc=1)
    own, p1, p2, p3 = first_sum(meta, keep, other)
    col = add4(
        own[0], along_inner(p1[0], dz=1), along_inner(p2[0], dz=2), along_inner(p3[0], dz=3), BF16
    )
    v2a = along_x(v3[:4], 1)
    v2b = along_x(v1[4:], 3)
    tile = add4(col, along_inner(col, dy=1), along_inner(col, dy=2), along_inner(col, dy=3), BF16)
    mine = (tile, along_inner(tile, dz=3), along_inner(tile, dz=2), along_inner(tile, dz=1))
    theirs = tuple(along_inner(x, dc=1) for x in mine)

    p, pn, sall = proj_part(meta, plan, mine + theirs, low_u, mix, lt)
    ikeep, isend = image_part(meta, plan, p, pn, (right_v, v1, v2a, v2b, v3))
    basis, inv = factor(meta, sall)

    iother = along_inner(isend, dc=1)
    own, p1, p2, p3 = first_sum(meta, ikeep, iother)
    own, p1, p2, p3 = second_sum(
        meta, own, along_inner(p1, dz=1), along_inner(p2, dz=2), along_inner(p3, dz=3)
    )
    image = finish(inv, own, along_inner(p1, dy=1), along_inner(p2, dy=2), along_inner(p3, dy=3))
    return (jnp.swapaxes(basis, 1, 2), jnp.swapaxes(image, 1, 2))


def solution(mesh):
    dev = P(("tgt", "inner"))
    return jax.shard_map(
        steps,
        mesh=mesh,
        in_specs=(dev,) * 10 + (P("tgt"),),
        out_specs=(P("tgt", None, "inner"), P("tgt", None, "inner")),
        check_vma=False,
    )
```

```python
import jax
import jax.numpy as jnp
from jax import lax
from jax.experimental import pallas as pl
from jax.experimental.pallas import tpu as pltpu
from jax.sharding import PartitionSpec as P


B = 1024
R = 64
MOD = 65521
N_LOW = 32
N_NEAR = 4
N_PAIR = N_LOW + N_NEAR
HALF = N_PAIR // 2
F32 = jnp.float32
BF16 = jnp.bfloat16


M_T = N_PAIR
M_COUNT = 2 * N_PAIR
M_CORE = M_COUNT + 1
M_Z = M_COUNT + 2
M_Y = M_COUNT + 3
M_S = M_COUNT + 4

SMEM = pl.BlockSpec(memory_space=pltpu.MemorySpace.SMEM)
VM = pl.BlockSpec(memory_space=pltpu.MemorySpace.VMEM)
ANY = pl.BlockSpec(memory_space=pltpu.MemorySpace.HBM)
PARAMS = pltpu.CompilerParams(vmem_limit_bytes=32 * 1024 * 1024)
SMALL = pltpu.CompilerParams(vmem_limit_bytes=12 * 1024 * 1024)


def in_hbm(*xs):
    return tuple(pltpu.with_memory_space_constraint(x, pltpu.MemorySpace.HBM) for x in xs)


def dot_nt(a, b):
    return lax.dot_general(a, b, (((1,), (1,)), ((), ())), preferred_element_type=F32)


def dot_nn(a, b):
    return lax.dot_general(a, b, (((1,), (0,)), ((), ())), preferred_element_type=F32)


def split2(x):
    hi = x.astype(BF16)
    return hi, (x - hi.astype(F32)).astype(BF16)


def zeta_kernel(req, v_ref, o0, o1, o2, o3, base, probe, tab):
    c = lax.broadcasted_iota(jnp.int32, (R, B), 0)
    i = lax.broadcasted_iota(jnp.int32, (R, B), 1)
    f = i * i * 7 + i * c * 131 + c * c * 17 + i * 7919 + c * 104729
    q = (f.astype(F32) * (1.0 / MOD)).astype(jnp.int32)
    f = f - q * MOD
    f = jnp.where(f < 0, f + MOD, f)
    f = jnp.where(f >= MOD, f - MOD, f)
    base[...] = f.astype(F32)
    v = v_ref[...].reshape(8 * R, B)
    left = lax.broadcasted_iota(jnp.int32, (4 * R, 128), 1) < R

    def batch(b, carry):
        row = b // 2
        for u in range(4):
            seed = req[row, 2 * N_PAIR + (b % 2) * 4 + u]
            shift = lax.rem(seed * 9973, MOD).astype(F32)
            code = base[...] + shift
            code = jnp.where(code >= MOD, code - MOD, code)
            probe[u * R : (u + 1) * R] = ((code - 32760.0) * (1.0 / 32768.0)).astype(BF16)
        res = dot_nt(probe[...], v)
        for ip in range(4):
            blk = res[:, ip * 128 : (ip + 1) * 128]
            rolled = pltpu.roll(blk, R, 1)
            even = jnp.where(left, blk, rolled)
            odd = jnp.where(left, rolled, blk)
            for u in range(4):
                tab[b * 4 + u, 2 * ip] = even[u * R : (u + 1) * R]
                tab[b * 4 + u, 2 * ip + 1] = odd[u * R : (u + 1) * R]
        return carry

    lax.fori_loop(0, 8, batch, 0)
    lm = lax.broadcasted_iota(jnp.int32, (R, 128), 1) < R

    def slot(p, carry):
        for q, out in enumerate((o0, o1, o2, o3)):
            ra = req[q, p] & 7
            ta = req[q, N_PAIR + p]
            rb = req[q, HALF + p] & 7
            tb = req[q, N_PAIR + HALF + p]
            out[p] = jnp.where(lm, tab[q * 8 + ta, ra], tab[q * 8 + tb, rb]).astype(BF16)
        return carry

    lax.fori_loop(0, HALF, slot, 0)


def zeta_home(req, v_own):
    out = jax.ShapeDtypeStruct((HALF, R, 128), BF16)
    return pl.pallas_call(
        zeta_kernel,
        out_shape=(out,) * 4,
        in_specs=[SMEM, VM],
        out_specs=(VM,) * 4,
        scratch_shapes=[
            pltpu.VMEM((R, B), F32),
            pltpu.VMEM((4 * R, B), BF16),
            pltpu.VMEM((32, 8, R, 128), F32),
        ],
        compiler_params=PARAMS,
        name="zeta_home",
    )(req, v_own)


PLUS_TILES = 4


def start_tile(r, own, dst, sem):
    for cond, ref, shift in own(r):

        @pl.when(cond)
        def _():
            pltpu.make_async_copy(ref.at[(r & 7) - shift], dst, sem).start()


def plan_kernel(meta, plan, count, place):
    for t in range(8):
        count[t] = 0

    def tally(j, carry):
        t = meta[M_T + j]
        count[t] = count[t] + 1
        return carry

    lax.fori_loop(0, N_LOW, tally, 0)

    def start(t, slot):
        place[t] = slot
        full = (count[t] + 3) // 4

        def mark(c, carry):
            plan[64 + slot // 4 + c] = t
            return carry

        lax.fori_loop(0, full, mark, 0)
        return slot + full * 4

    plan[127] = lax.fori_loop(0, 8, start, 0)

    def put(j, carry):
        t = meta[M_T + j]
        at = place[t]
        plan[at] = j + 256
        place[t] = at + 1
        return carry

    lax.fori_loop(0, N_LOW, put, 0)

    def pad(t, carry):
        end = place[t]

        def fill(i, carry):
            plan[i] = plan[end - 1] & 255
            return carry

        return lax.fori_loop(end, (end + 3) // 4 * 4, fill, carry)

    lax.fori_loop(0, 8, pad, 0)


def make_plan(meta):
    return pl.pallas_call(
        plan_kernel,
        out_shape=jax.ShapeDtypeStruct((128,), jnp.int32),
        in_specs=[SMEM],
        out_specs=SMEM,
        scratch_shapes=[pltpu.SMEM((8,), jnp.int32), pltpu.SMEM((8,), jnp.int32)],
        compiler_params=SMALL,
        name="make_plan",
    )(meta)


def left_body(meta, mine, own, lv, nt, mix, lt, lst, lvb, ub, nb, unb, sems, nsems, value=None):
    def low(j, n):
        r = meta[j]
        hit = mine(r >> 3)

        @pl.when(hit)
        def _():
            lst[n] = j
            pltpu.make_async_copy(lv.at[j], lvb.at[n], sems.at[0, n]).start()
            if value is None:
                start_tile(r, own, ub.at[n], sems.at[1, n])

        return n + hit.astype(jnp.int32)

    n = lax.fori_loop(0, N_LOW, low, 0)

    def near(s, m):
        r = meta[N_LOW + s]
        hit = mine(r >> 3) & (s < meta[M_COUNT])

        @pl.when(hit)
        def _():
            lst[N_LOW + m] = s
            pltpu.make_async_copy(nt.at[s], nb.at[m], nsems.at[0, m]).start()
            if value is None:
                start_tile(r, own, unb.at[m], nsems.at[1, m])

        return m + hit.astype(jnp.int32)

    nn = lax.fori_loop(0, N_NEAR, near, 0)

    def group(g, carry):
        for i in range(4):
            pos = g * 4 + i

            @pl.when(pos < n)
            def _():
                pltpu.make_async_copy(lv.at[0], lvb.at[pos], sems.at[0, pos]).wait()
                if value is None:
                    pltpu.make_async_copy(lv.at[0], ub.at[pos], sems.at[1, pos]).wait()

        spots = [jnp.minimum(g * 4 + i, n - 1) for i in range(4)]
        tiles = [ub[pos] if value is None else value(meta[lst[pos]]) for pos in spots]
        done = [dot_nt(u, lvb[pos]) for u, pos in zip(tiles, spots)]
        for pos, mt in zip(spots, done):
            mix[lst[pos]] = jnp.concatenate([mt, mt], axis=1).astype(BF16)
        return carry

    lax.fori_loop(0, (n + 3) // 4, group, 0)

    def tile(m, carry):
        pltpu.make_async_copy(nt.at[0], nb.at[m], nsems.at[0, m]).wait()
        at = lst[N_LOW + m]
        if value is None:
            pltpu.make_async_copy(lv.at[0], unb.at[m], nsems.at[1, m]).wait()
        u = unb[m] if value is None else value(meta[N_LOW + at])
        lt[at] = dot_nt(u, nb[m]).astype(BF16)
        return carry

    lax.fori_loop(0, nn, tile, 0)


def sum_body(meta, mine, zbuf, lu, mix, lt, acc, lst, lub, sems):
    def low(j, n):
        hit = mine(meta[j] >> 3)

        @pl.when(hit)
        def _():
            lst[n] = j
            pltpu.make_async_copy(lu.at[j], lub.at[n], sems.at[n]).start()

        return n + hit.astype(jnp.int32)

    n = lax.fori_loop(0, N_LOW, low, 0)

    def zeta(j):
        second = j >= HALF
        blk = zbuf[meta[j] >> 3, jnp.where(second, j - HALF, j)].astype(F32)
        return jnp.where(second, pltpu.roll(blk, R, 1), blk)[:, :R].astype(BF16)

    def tile(s, carry):
        @pl.when(mine(meta[N_LOW + s] >> 3))
        def _():
            acc[meta[M_T + N_LOW + s]] += dot_nn(zeta(N_LOW + s), lt[s])

        return carry

    lax.fori_loop(0, meta[M_COUNT], tile, 0)

    left = lax.broadcasted_iota(jnp.int32, (R, 2 * R), 1) < R

    def group(g, carry):
        terms = []
        for i in range(4):
            pos = jnp.minimum(g * 4 + i, n - 1)
            j = lst[pos]
            w = dot_nn(zeta(j), mix[j]) * (g * 4 + i < n).astype(F32)
            hi = w.astype(BF16).astype(F32)
            terms.append((pos, j, jnp.where(left, hi, w - hi).astype(BF16)))
        for i in range(4):
            pos = g * 4 + i

            @pl.when(pos < n)
            def _():
                pltpu.make_async_copy(lu.at[0], lub.at[pos], sems.at[pos]).wait()

        for pos, j, w in terms:
            tile = lub[pos]
            acc[meta[M_T + j]] += dot_nn(w, jnp.concatenate([tile, tile], axis=0))
        return carry

    lax.fori_loop(0, (n + 3) // 4, group, 0)


N_LEFT = 7


def pairs_0_kernel(meta, u0, z0, lv, lu, nt, acc, mix, lt, zbuf, *scratch):
    acc[...] = jnp.zeros_like(acc)
    zbuf[0] = z0[...]
    mine = lambda rel: rel == 0
    left_body(meta, mine, lambda r: ((r >= 0, u0, 0),), lv, nt, mix, lt, *scratch[:N_LEFT])
    sum_body(meta, mine, zbuf, lu, mix, lt, acc, *scratch[N_LEFT:])


def near_side(rel):
    return (rel == 1) | (rel == 3)


def far_side(rel):
    return rel == 2


def left_a_kernel(meta, u1, u3, mix_in, lt_in, lv, nt, mix, lt, *scratch):
    mix[...] = mix_in[...]
    lt[...] = lt_in[...]
    left_body(
        meta, near_side, lambda r: ((r < 16, u1, 0), (r >= 16, u3, 0)), lv, nt, mix, lt, *scratch
    )


def left_b_kernel(meta, u2a, u2b, mix_in, lt_in, lv, nt, mix, lt, *scratch):
    def value(r):
        i = r & 7
        first = u2a[jnp.minimum(i, PLUS_TILES - 1)]
        return jnp.where(i < PLUS_TILES, first, u2b[jnp.maximum(i - PLUS_TILES, 0)])

    mix[...] = mix_in[...]
    lt[...] = lt_in[...]
    left_body(meta, far_side, None, lv, nt, mix, lt, *scratch, value=value)


def sum_a_kernel(meta, z1, z3, acc_in, mix, lt, lu, acc, zbuf, *scratch):
    acc[...] = acc_in[...]
    zbuf[1] = z1[...]
    zbuf[3] = z3[...]
    sum_body(meta, near_side, zbuf, lu, mix, lt, acc, *scratch)


def sum_b_kernel(meta, z2, acc_in, mix, lt, lu, keep, send, zbuf, acc, *scratch):
    acc[...] = acc_in[...]
    zbuf[2] = z2[...]
    sum_body(meta, far_side, zbuf, lu, mix, lt, acc, *scratch)
    core = meta[M_CORE]
    keep[...] = acc[pl.ds(core * 4, 4)]
    send[...] = acc[pl.ds(4 - core * 4, 4)]


ACC = jax.ShapeDtypeStruct((8, R, B), F32)
MIX = jax.ShapeDtypeStruct((N_LOW, R, 2 * R), BF16)
LEFT = jax.ShapeDtypeStruct((N_NEAR, R, B), BF16)
QUAD = jax.ShapeDtypeStruct((4, R, B), F32)
LEFT_SCRATCH = [
    pltpu.SMEM((N_PAIR,), jnp.int32),
    pltpu.VMEM((N_LOW, R, B), BF16),
    pltpu.VMEM((N_LOW, R, B), BF16),
    pltpu.VMEM((N_NEAR, B, B), BF16),
    pltpu.VMEM((N_NEAR, R, B), BF16),
    pltpu.SemaphoreType.DMA((2, N_LOW)),
    pltpu.SemaphoreType.DMA((2, N_NEAR)),
]
SUM_SCRATCH = [
    pltpu.SMEM((N_LOW,), jnp.int32),
    pltpu.VMEM((N_LOW, R, B), BF16),
    pltpu.SemaphoreType.DMA((N_LOW,)),
]
ZBUF = pltpu.VMEM((4, HALF, R, 128), BF16)


def pairs_0(meta, u0, z0, low_v, low_u, near):
    return pl.pallas_call(
        pairs_0_kernel,
        out_shape=(ACC, MIX, LEFT),
        in_specs=[SMEM, ANY, VM] + [ANY] * 3,
        out_specs=(VM, VM, VM),
        scratch_shapes=[ZBUF] + LEFT_SCRATCH + SUM_SCRATCH,
        compiler_params=PARAMS,
        name="pairs_0",
    )(meta, *in_hbm(u0), z0, *in_hbm(low_v, low_u, near))


def left_part(kernel, meta, us, mix, lt, low_v, near, in_place):
    return pl.pallas_call(
        kernel,
        out_shape=(MIX, LEFT),
        in_specs=[SMEM] + [VM if in_place else ANY] * 2 + [VM] * 2 + [ANY] * 2,
        out_specs=(VM, VM),
        scratch_shapes=LEFT_SCRATCH,
        compiler_params=PARAMS,
    )(meta, *(us if in_place else in_hbm(*us)), mix, lt, *in_hbm(low_v, near))


def sum_a(meta, z1, z3, acc, mix, lt, low_u):
    return pl.pallas_call(
        sum_a_kernel,
        out_shape=ACC,
        in_specs=[SMEM] + [VM] * 5 + [ANY],
        out_specs=VM,
        scratch_shapes=[ZBUF] + SUM_SCRATCH,
        compiler_params=PARAMS,
        name="sum_a",
    )(meta, z1, z3, acc, mix, lt, *in_hbm(low_u))


def sum_b(meta, z2, acc, mix, lt, low_u):
    return pl.pallas_call(
        sum_b_kernel,
        out_shape=(QUAD, QUAD),
        in_specs=[SMEM] + [VM] * 4 + [ANY],
        out_specs=(VM, VM),
        scratch_shapes=[ZBUF, pltpu.VMEM((8, R, B), F32)] + SUM_SCRATCH,
        compiler_params=PARAMS,
        name="sum_b",
    )(meta, z2, acc, mix, lt, *in_hbm(low_u))


SLOTS = 56


def proj_kernel(
    meta, plan, s0, s1, s2, s3, r0, r1, r2, r3, lu, mix, lt, p_ref, pn_ref, sall, lub, sems
):
    count = plan[127]

    def load(i, carry):
        pltpu.make_async_copy(lu.at[plan[i] & 255], lub.at[i], sems.at[i]).start()
        return carry

    lax.fori_loop(0, count, load, 0)
    core = meta[M_CORE]
    z = meta[M_Z]
    for n, ref in enumerate((s0, s1, s2, s3)):
        sall[core * 4 + ((z + n) & 3)] = ref[...]
    for n, ref in enumerate((r0, r1, r2, r3)):
        sall[(1 - core) * 4 + ((z + n) & 3)] = ref[...]

    for s in range(N_NEAR):
        pn_ref[s] = dot_nt(sall[meta[M_T + N_LOW + s]], lt[s]).astype(BF16)
    n = count // 4

    def ready(m):
        @pl.when(m < n)
        def _():
            for i in range(4):
                at = m * 4 + i
                pltpu.make_async_copy(lu.at[0], lub.at[at], sems.at[at]).wait()

    left = lax.broadcasted_iota(jnp.int32, (R, 2 * R), 1) < R
    none = jnp.zeros((R, 2 * R), BF16)

    def chunk(m):
        at = m * 4
        q = dot_nt(sall[plan[64 + m]], lub[pl.ds(at, 4)].reshape(4 * R, B))
        rows = []
        for i in range(4):
            e = plan[at + i]
            use = (left if i % 2 == 0 else jnp.logical_not(left)) & (e >= 256)
            blk = jnp.where(use, mix[e & 255].astype(F32), 0.0).astype(BF16)
            rows.append(jnp.concatenate([blk, none] if i < 2 else [none, blk], axis=1))
        both = dot_nt(jnp.concatenate(split2(q), axis=0), jnp.concatenate(rows, axis=0))
        return (both[:R] + both[R:]).astype(BF16)

    def two(i, carry):
        m0 = 2 * i
        m1 = jnp.minimum(m0 + 1, n - 1)
        ready(m0)
        ready(m0 + 1)
        p0 = chunk(m0)
        p1 = chunk(m1)
        p_ref[m0] = p0
        p_ref[m1] = p1
        return carry

    lax.fori_loop(0, (n + 1) // 2, two, 0)


def image_kernel(meta, plan, p_ref, pn_ref, v0, v1, v2a, v2b, v3, keep, send, vb, nvb, acc, sems, nsems):
    def fetch(r, buf, i, sem):
        rel = r >> 3
        k = r & 7
        for n, ref in ((0, v0), (1, v1), (3, v3)):

            @pl.when(rel == n)
            def _():
                pltpu.make_async_copy(ref.at[k], buf.at[i], sem).start()

        @pl.when((rel == 2) & (k < 4))
        def _():
            buf[i] = v2a[k & 3]

        @pl.when((rel == 2) & (k >= 4))
        def _():
            buf[i] = v2b[k & 3]

    def arrived(r, buf, i, sem):
        @pl.when((r >> 3) != 2)
        def _():
            pltpu.make_async_copy(v0.at[0], buf.at[i], sem).wait()

    count = plan[127]

    def load(i, carry):
        fetch(meta[plan[i] & 255], vb, i, sems.at[i])
        return carry

    lax.fori_loop(0, count, load, 0)

    def nload(s, carry):
        fetch(meta[N_LOW + s], nvb, s, nsems.at[s])
        return carry

    lax.fori_loop(0, meta[M_COUNT], nload, 0)
    acc[...] = jnp.zeros_like(acc)

    def chunk(m, carry):
        at = m * 4
        for i in range(4):
            arrived(meta[plan[at + i] & 255], vb, at + i, sems.at[at + i])
        acc[plan[64 + m]] += dot_nn(p_ref[m], vb[pl.ds(at, 4)].reshape(4 * R, B))
        return carry

    lax.fori_loop(0, count // 4, chunk, 0)

    def near(s, carry):
        arrived(meta[N_LOW + s], nvb, s, nsems.at[s])
        acc[meta[M_T + N_LOW + s]] += dot_nn(pn_ref[s], nvb[s])
        return carry

    lax.fori_loop(0, meta[M_COUNT], near, 0)
    flip = acc[...].astype(BF16).reshape(8 * R, B).T.reshape(16, 2, 32, 8 * R)
    first = meta[M_CORE] == 0

    @pl.when(first)
    def _():
        keep[...] = flip[:, 0]
        send[...] = flip[:, 1]

    @pl.when(jnp.logical_not(first))
    def _():
        keep[...] = flip[:, 1]
        send[...] = flip[:, 0]


def proj_part(meta, plan, tiles, low_u, mix, lt):
    return pl.pallas_call(
        proj_kernel,
        out_shape=(
            jax.ShapeDtypeStruct((SLOTS // 4, R, 4 * R), BF16),
            jax.ShapeDtypeStruct((N_NEAR, R, R), BF16),
            jax.ShapeDtypeStruct((8, R, B), BF16),
        ),
        in_specs=[SMEM, SMEM] + [VM] * 8 + [ANY] + [VM] * 2,
        out_specs=(VM,) * 3,
        scratch_shapes=[pltpu.VMEM((SLOTS, R, B), BF16), pltpu.SemaphoreType.DMA((SLOTS,))],
        compiler_params=PARAMS,
        name="proj_part",
    )(meta, plan, *tiles, *in_hbm(low_u), mix, lt)


def image_part(meta, plan, p, pn, vs):
    half = jax.ShapeDtypeStruct((16, 32, 8 * R), BF16)
    return pl.pallas_call(
        image_kernel,
        out_shape=(half, half),
        in_specs=[SMEM, SMEM, VM, VM, ANY, ANY, VM, VM, ANY],
        out_specs=(VM,) * 2,
        scratch_shapes=[
            pltpu.VMEM((SLOTS, R, B), BF16),
            pltpu.VMEM((N_NEAR, R, B), BF16),
            pltpu.VMEM((8, R, B), F32),
            pltpu.SemaphoreType.DMA((SLOTS,)),
            pltpu.SemaphoreType.DMA((N_NEAR,)),
        ],
        compiler_params=PARAMS,
        name="image_part",
    )(meta, plan, p, pn, *in_hbm(*vs[:2]), *vs[2:4], *in_hbm(vs[4]))


def dot_exact(a, b):
    return lax.dot_general(
        a, b, (((1,), (1,)), ((), ())), precision=lax.Precision.HIGHEST, preferred_element_type=F32
    )


def eliminate(m, ks):
    for k in ks:
        r0 = k // 8 * 8
        block = m[:, r0:, :]
        piv = m[:, k : k + 1, :]
        scaled = piv * (1.0 / piv[:, :, k : k + 1])
        fac = block[:, :, k : k + 1]
        if r0 + 8 > k:
            rows = lax.broadcasted_iota(jnp.int32, fac.shape, 1) + r0
            fac = jnp.where(rows > k, fac, 0.0)
        m[:, r0:, :] = block - fac * scaled


def factor_0_kernel(meta, s_ref, m, cols):
    lane = lax.broadcasted_iota(jnp.int32, (R, 2 * R), 1)
    row = lax.broadcasted_iota(jnp.int32, (R, 2 * R), 0)
    eye = (lane == row + R).astype(F32)
    pick_row = lax.broadcasted_iota(jnp.int32, (32, B), 0) + meta[M_S] * 32
    pick = (lax.broadcasted_iota(jnp.int32, (32, B), 1) == pick_row).astype(BF16)
    for t in range(8):
        s = s_ref[t]
        g = dot_nt(jnp.concatenate([s, pick], axis=0), s)
        m[t] = jnp.where(lane < R, jnp.concatenate([g[:R], g[:R]], axis=1), eye)
        cols[t] = g[R:]
    eliminate(m, range(CUT0))


def factor_1_kernel(m_in, m):
    m[...] = m_in[...]
    eliminate(m, range(CUT0, CUT1))


def factor_2_kernel(m_in, cols, basis, inv, m):
    m[...] = m_in[...]
    eliminate(m, range(CUT1, R))
    lane = lax.broadcasted_iota(jnp.int32, (R, 2 * R), 1)
    row = lax.broadcasted_iota(jnp.int32, (R, 2 * R), 0)
    for t in range(8):
        a = m[t]
        diag = jnp.sum(jnp.where(lane == row, a, 0.0), axis=1, keepdims=True)
        li = a[:, R:] * lax.rsqrt(diag)
        inv[t] = li
        basis[t] = 32.0 * dot_exact(cols[t], li)


CUT0 = 8
CUT1 = 48
STATE = jax.ShapeDtypeStruct((8, R, 2 * R), F32)
COLS = jax.ShapeDtypeStruct((8, 32, R), F32)


def factor(meta, s):
    m, cols = pl.pallas_call(
        factor_0_kernel,
        out_shape=(STATE, COLS),
        in_specs=[SMEM, VM],
        out_specs=(VM, VM),
        compiler_params=SMALL,
        name="factor_0",
    )(meta, s)
    m = pl.pallas_call(
        factor_1_kernel, out_shape=STATE, in_specs=[VM], out_specs=VM, compiler_params=SMALL, name="factor_1"
    )(m)
    return pl.pallas_call(
        factor_2_kernel,
        out_shape=(COLS, jax.ShapeDtypeStruct((8, R, R), F32)),
        in_specs=[VM, VM],
        out_specs=(VM, VM),
        scratch_shapes=[pltpu.VMEM((8, R, 2 * R), F32)],
        compiler_params=SMALL,
        name="factor_2",
    )(m, cols)


def first_sum(meta, a, b):
    part = (a.shape[0] // 4,) + a.shape[1:]
    n = part[0]

    def body(meta, a, b, own, p1, p2, p3):
        z = meta[M_Z]
        for k, out in enumerate((own, p1, p2, p3)):
            at = pl.ds(((z + k) & 3) * n, n)
            out[...] = (a[at].astype(F32) + b[at].astype(F32)).astype(out.dtype)

    outs = pl.pallas_call(
        body,
        out_shape=(jax.ShapeDtypeStruct(part, F32),) + (jax.ShapeDtypeStruct(part, BF16),) * 3,
        in_specs=[SMEM, VM, VM],
        out_specs=(VM,) * 4,
        compiler_params=SMALL,
        name="first_sum",
    )(meta, a, b)
    return outs


def add4(a, b, c, d, dtype):
    def body(a, b, c, d, out):
        out[...] = (a[...].astype(F32) + b[...].astype(F32) + c[...].astype(F32) + d[...].astype(F32)).astype(dtype)

    return pl.pallas_call(
        body,
        out_shape=jax.ShapeDtypeStruct(a.shape, dtype),
        in_specs=[VM] * 4,
        out_specs=VM,
        compiler_params=SMALL,
    )(a, b, c, d)


def second_sum(meta, a, b, c, d):
    shape = a.shape[1:]

    def body(meta, a, b, c, d, own, p1, p2, p3):
        y = meta[M_Y]
        for k, out in enumerate((own, p1, p2, p3)):
            at = (y + k) & 3
            out[...] = a[at] + b[at].astype(F32) + c[at].astype(F32) + d[at].astype(F32)

    return pl.pallas_call(
        body,
        out_shape=(jax.ShapeDtypeStruct(shape, F32),) * 4,
        in_specs=[SMEM] + [VM] * 4,
        out_specs=(VM,) * 4,
        compiler_params=SMALL,
        name="second_sum",
    )(meta, a, b, c, d)


def finish(inv, a, b, c, d):
    def body(inv, a, b, c, d, out):
        total = a[...] + b[...] + c[...] + d[...]
        for t in range(8):
            out[t] = dot_exact(total[:, t * R : (t + 1) * R], inv[t])

    return pl.pallas_call(
        body,
        out_shape=jax.ShapeDtypeStruct((8, 32, R), F32),
        in_specs=[VM] * 5,
        out_specs=VM,
        compiler_params=SMALL,
        name="finish",
    )(inv, a, b, c, d)


def along_x(x, step):
    return lax.ppermute(x, "tgt", [(i, (i + step) % 4) for i in range(4)])


def along_inner(x, dz=0, dy=0, dc=0):
    pairs = []
    for z in range(4):
        for y in range(4):
            for c in range(2):
                to = (((z + dz) % 4) * 4 + (y + dy) % 4) * 2 + (c ^ dc)
                pairs.append(((z * 4 + y) * 2 + c, to))
    return lax.ppermute(x, "inner", pairs)


def after(x, *others):
    return lax.optimization_barrier((x,) + others)[0]


def steps(
    near_tiles, near_target, near_right, near_count, low_u, low_v, low_target, low_right, right_u, right_v, probe_seed
):
    g = lax.axis_index("tgt")
    s = lax.axis_index("inner")
    rights = jnp.concatenate([low_right, near_right])
    targets = jnp.concatenate([low_target, near_target])
    req = jnp.concatenate([rights, targets, probe_seed, jnp.zeros((128 - 2 * N_PAIR - 8,), jnp.int32)])[None]
    place = jnp.stack([near_count[0], s & 1, s >> 3, (s >> 1) & 3, s]).astype(jnp.int32)
    meta = jnp.concatenate(
        [(rights - 8 * g) & 31, targets, place, jnp.zeros((128 - 2 * N_PAIR - 5,), jnp.int32)]
    )

    u3 = along_x(right_u, 1)
    u1 = along_x(right_u, 3)
    reqs = jnp.concatenate([req, along_x(req, 3), along_x(req, 2), along_x(req, 1)])
    o0, o1, o2, o3 = zeta_home(after(reqs, meta), right_v)
    z1 = along_x(o3, 3)
    z3 = along_x(o1, 1)
    u2a = along_x(u3[:PLUS_TILES], 1)
    u2b = along_x(u1[PLUS_TILES:], 3)
    v3 = along_x(right_v, 1)
    v1 = along_x(right_v, 3)

    acc, mix, lt = pairs_0(meta, right_u, o0, low_v, low_u, near_tiles)
    z2 = along_x(o2, 2)
    mix, lt = left_part(left_a_kernel, meta, (u1, u3), mix, lt, low_v, near_tiles, False)
    acc = sum_a(meta, z1, z3, acc, mix, lt, low_u)
    mix, lt = left_part(left_b_kernel, meta, (u2a, u2b), mix, lt, low_v, near_tiles, True)
    keep, send = sum_b(meta, z2, acc, mix, lt, low_u)

    plan = make_plan(after(meta, keep))

    other = along_inner(send, dc=1)
    own, p1, p2, p3 = first_sum(meta, keep, other)
    col = add4(
        own[0], along_inner(p1[0], dz=1), along_inner(p2[0], dz=2), along_inner(p3[0], dz=3), BF16
    )
    v2a = along_x(v3[:4], 1)
    v2b = along_x(v1[4:], 3)
    tile = add4(col, along_inner(col, dy=1), along_inner(col, dy=2), along_inner(col, dy=3), BF16)
    mine = (tile, along_inner(tile, dz=3), along_inner(tile, dz=2), along_inner(tile, dz=1))
    theirs = tuple(along_inner(x, dc=1) for x in mine)

    p, pn, sall = proj_part(meta, plan, mine + theirs, low_u, mix, lt)
    ikeep, isend = image_part(meta, plan, p, pn, (right_v, v1, v2a, v2b, v3))
    basis, inv = factor(meta, sall)

    iother = along_inner(isend, dc=1)
    own, p1, p2, p3 = first_sum(meta, ikeep, iother)
    own, p1, p2, p3 = second_sum(
        meta, own, along_inner(p1, dz=1), along_inner(p2, dz=2), along_inner(p3, dz=3)
    )
    image = finish(inv, own, along_inner(p1, dy=1), along_inner(p2, dy=2), along_inner(p3, dy=3))
    return (jnp.swapaxes(basis, 1, 2), jnp.swapaxes(image, 1, 2))


def solution(mesh):
    dev = P(("tgt", "inner"))
    return jax.shard_map(
        steps,
        mesh=mesh,
        in_specs=(dev,) * 10 + (P("tgt"),),
        out_specs=(P("tgt", None, "inner"), P("tgt", None, "inner")),
        check_vma=False,
    )
```
